32 devices in a mesh: feat: 2 (over y), node: 16 (over z, x, core).
Axes of the slice: x: 2, y: 2, z: 4, core: 2. Of those that a mesh axis runs over, the one named last changes fastest.
Arguments:
- features: bfloat16 [32768, 4096], P('node', 'feat'), may hold values from -6 to 6
- seed_feats: bfloat16 [2048, 4096], P('node', 'feat'), may hold values from -6 to 6
- patterns: int32 [256, 8, 128, 8], P('node'), may hold values from 0 to 65535, as said below
- sources: int32 [256, 8], P('node'), may hold values from 0 to 15
- counts: int32 [256], P('node'), may hold values from 1 to 8
- w_self: bfloat16 [4096, 1024], P('feat'), may hold values from -0.09375 to 0.09375
- w_neigh: bfloat16 [4096, 1024], P('feat'), may hold values from -0.09375 to 0.09375
- bias_term: float32 [1024], replicated, may hold values from -3 to 3
- out_grad: bfloat16 [2048, 1024], P('node'), may hold values from -0.5 to 0.5
Outputs:
- hidden: bfloat16 [2048, 1024], P('node')
- grad_self: float32 [4096, 1024], P(('feat', 'node'))
- grad_neigh: float32 [4096, 1024], P(('feat', 'node'))
- grad_bias: float32 [1024], P('node')
The draws below stay inside these ranges and needn't reach their ends.
Inputs may be any that keep to these rules, and one draw needn't show every extreme that they name: `patterns`: each word holds 16 entries of 0 or 1 in its 16 low bits.
All inputs are finite; a program needn't handle non-finite values.
Results may differ from the reference program's by a relative error of at most 0.024.
The reference program's roundings to bfloat16 on the way count: a program that leaves them out, or rounds other values in their place, can miss the bound.
Values may be sent and summed in bfloat16 or wider, within the bound.
A program may use at most 128 MiB of HBM per device.

```python
import jax
import jax.numpy as jnp
from jax import lax

D = 4096
HID = 1024
BLK = 128
WORDS = 8
FAN = 8
NB_DEV = 16
SEED_BLOCKS = 16
SEEDS = 2048
NODES = 32768
LISTS = 256
N_NODE = 16


def draw_patterns(key, part):
    key_first, key_second = jax.random.split(key)
    pattern_shape = (LISTS, FAN, BLK, WORDS)
    first_bits = jax.random.randint(key_first, pattern_shape, 0, 65536, dtype=jnp.int32)
    second_bits = jax.random.randint(key_second, pattern_shape, 0, 65536, dtype=jnp.int32)
    packed = jnp.bitwise_and(first_bits, second_bits)
    return packed.at[0, 0, 0, 0].set(65535)


def draw_counts(key, part):
    groups = LISTS // SEED_BLOCKS
    key_level, key_place = jax.random.split(key)
    group_rank = jnp.arange(groups, dtype=jnp.int32)[:, None]
    count_level = 2 + (FAN - 2) * group_rank // max(groups - 1, 1)
    random_bits = jax.random.randint(key_level, (groups, SEED_BLOCKS), 0, 1048576, dtype=jnp.int32)
    drawn = 1 + random_bits % count_level
    forced_at = jax.random.randint(key_place, (), 0, SEED_BLOCKS, dtype=jnp.int32)
    drawn = drawn.at[groups - 1, forced_at].set(FAN)
    return drawn.reshape(LISTS).astype(jnp.int32)


def place_ends(values, own_key, smallest, high):
    dims = values.shape
    place = [jax.random.randint(jax.random.fold_in(own_key, axis), (), 0, dims[axis]) for axis in range(len(dims))]
    values = values.at[tuple(place)].set(smallest)
    longest = dims.index(max(dims))
    place[longest] = (place[longest] + 1) % dims[longest]
    return values.at[tuple(place)].set(high)


def with_spikes(entries, stream_key, source, target, shards_of, factor):
    owner, partner = [(jnp.arange(entries.shape[dim]) // (entries.shape[dim] // shards_of)).reshape([-1 if axis == dim else 1 for axis in range(entries.ndim)]) for dim in (source, target)]
    chosen = jax.random.permutation(stream_key, shards_of)[partner]
    strong = (owner == chosen) | (owner == (partner + shards_of // 2) % shards_of)
    return jnp.where(strong, factor * entries, entries)


def shard_levels(key, dims, cuts, smallest, largest):
    level = 1.0
    for dim, blocks in cuts:
        draws = jax.random.uniform(jax.random.fold_in(jax.random.fold_in(key, 6), dim), (blocks,), jnp.float32, smallest / len(cuts), largest / len(cuts))
        level = level * jnp.repeat(jnp.exp(draws), dims[dim] // blocks).reshape((-1,) + (1,) * (len(dims) - 1 - dim))
    return level


def bell_draw(own_key, shape, width, reach, pieces=(), kind=jnp.bfloat16):
    values = jax.random.normal(own_key, shape, jnp.float32) * width
    if len(pieces) > 0:
        values = shard_levels(own_key, shape, pieces, -0.22, 0.18) * values
    return jnp.clip(values, min=-reach, max=reach).astype(kind)


def heavy_noise(stream_key, extent, spread, bound, cuts, heavy, held_as=jnp.bfloat16):
    entries = spread * jax.random.normal(stream_key, extent, jnp.float32)
    if cuts:
        entries = entries * shard_levels(stream_key, extent, cuts, -0.22, 0.18)
    return jnp.clip(with_spikes(entries, jax.random.fold_in(stream_key, 3), *heavy), -bound, bound).astype(held_as)


def setup_inputs(seed: int = 0) -> dict:
    seeds = jax.random.split(jax.random.key(seed), 10)
    features = bell_draw(seeds[0], (NODES, D), 1.0, 6.0, ((0, 16), (1, 2)))
    seed_feats = heavy_noise(seeds[1], (SEEDS, D), 1.0, 6.0, ((0, 16), (1, 2)), (0, 1, 16, 2.0))
    patterns = draw_patterns(jax.random.fold_in(seeds[9], 71), 0)
    sources = place_ends(jax.random.randint(seeds[3], (LISTS, FAN), 0, NB_DEV), jax.random.fold_in(seeds[3], 1), 0, NB_DEV - 1).astype(jnp.int32)
    counts = draw_counts(jax.random.fold_in(seeds[9], 71), 0)
    w_self = bell_draw(seeds[5], (D, HID), D ** -0.5, 0.09375, ((0, 2),))
    w_neigh = bell_draw(seeds[6], (D, HID), D ** -0.5, 0.09375, ((0, 2),))
    bias_term = bell_draw(seeds[7], (HID,), 0.5, 3.0, (), jnp.float32)
    out_grad = bell_draw(seeds[8], (SEEDS, HID), ((SEEDS // 2) ** -0.5), 0.5, ((0, 16),))
    return dict(features=features, seed_feats=seed_feats, patterns=patterns, sources=sources, counts=counts, w_self=w_self, w_neigh=w_neigh, bias_term=bias_term, out_grad=out_grad)


def unpack(packed):
    shifts = jnp.arange(16, dtype=jnp.int32)
    bit_values = jnp.bitwise_and(jnp.right_shift(packed[..., None], shifts), 1)
    return bit_values.reshape(packed.shape[:-1] + (packed.shape[-1] * 16,)).astype(jnp.float32)

def reference(features, seed_feats, patterns, sources, counts, w_self, w_neigh, bias_term, out_grad):
    feature_blocks = features.reshape(N_NODE, NB_DEV, BLK, D)
    pattern_rows = patterns.reshape(N_NODE, SEED_BLOCKS, FAN, BLK, WORDS)
    source_rows = sources.reshape(N_NODE, SEED_BLOCKS, FAN)
    count_rows = counts.reshape(N_NODE, SEED_BLOCKS)

    def one_source(state_pair, inputs):
        summed_rows, degree = state_pair
        block_feats, group_patterns, group_sources, group_counts = inputs
        live_mask = jnp.arange(FAN, dtype=jnp.int32)[None, :] < group_counts[:, None]
        for slot_index in range(FAN):
            tile_now = unpack(group_patterns[:, slot_index]) * live_mask[:, slot_index, None, None].astype(jnp.float32)
            chosen = block_feats[group_sources[:, slot_index]].astype(jnp.float32)
            summed_rows = summed_rows + jnp.einsum('trs,tsd->trd', tile_now, chosen)
            degree = degree + lax.optimization_barrier(jnp.sum(tile_now, axis=2))
        return ((summed_rows, degree), None)
    start_state = (jnp.zeros((SEED_BLOCKS, BLK, D), jnp.float32), jnp.zeros((SEED_BLOCKS, BLK), jnp.float32))
    (summed_rows, degree), _ = lax.scan(one_source, start_state, (feature_blocks, pattern_rows, source_rows, count_rows))
    aggregate = (summed_rows / jnp.sqrt(1.0 + degree)[:, :, None]).reshape(SEEDS, D).astype(jnp.bfloat16)
    pre_act = jnp.dot(seed_feats, w_self, preferred_element_type=jnp.float32)
    pre_act = pre_act + jnp.dot(aggregate, w_neigh, preferred_element_type=jnp.float32) + bias_term
    hidden = jnp.maximum(pre_act, 0.0).astype(jnp.bfloat16)
    grad_rows = jnp.where(pre_act > 0.0, out_grad, jnp.zeros_like(out_grad))
    grad_self = jnp.dot(seed_feats.T, grad_rows, preferred_element_type=jnp.float32)
    grad_neigh = jnp.dot(aggregate.T, grad_rows, preferred_element_type=jnp.float32)
    grad_bias = lax.optimization_barrier(jnp.sum(grad_rows.astype(jnp.float32), axis=0))
    return (hidden, grad_self, grad_neigh, grad_bias)
```

```python
import jax
import jax.numpy as jnp
from jax import lax
from jax.sharding import PartitionSpec as P


def unpack(packed):
    shifts = jnp.arange(16, dtype=jnp.int32)
    bit_values = jnp.bitwise_and(jnp.right_shift(packed[..., None], shifts), 1)
    return bit_values.reshape(packed.shape[:-1] + (packed.shape[-1] * 16,)).astype(jnp.bfloat16)


def body(features, seed_feats, patterns, sources, counts, w_self, w_neigh, bias_term, out_grad):
    targets = patterns.shape[0]
    fan_slots = patterns.shape[1]
    block_rows = patterns.shape[2]
    local_blocks = features.shape[0] // block_rows
    n_node = lax.axis_size("node")
    node_idx = lax.axis_index("node")
    live_mask = jnp.arange(fan_slots, dtype=jnp.int32)[None, :] < counts[:, None]
    tile_bits = unpack(patterns) * live_mask[:, :, None, None].astype(jnp.bfloat16)
    source_pick = (
        sources[:, :, None] == jnp.arange(local_blocks, dtype=jnp.int32)[None, None, :]
    ).astype(jnp.bfloat16)
    mixing = jnp.einsum(
        "tkrs,tkb->trbs", tile_bits, source_pick, preferred_element_type=jnp.bfloat16
    )
    mixing = mixing.reshape(targets * block_rows, local_blocks * block_rows)
    summed_rows = jnp.dot(mixing, features, preferred_element_type=jnp.float32)
    degree = jnp.sum(mixing, axis=1, dtype=jnp.float32)
    owner_sums = lax.psum_scatter(summed_rows, "node", scatter_dimension=0, tiled=True)
    owner_counts = lax.psum_scatter(degree, "node", scatter_dimension=0, tiled=True)
    aggregate = (owner_sums / jnp.sqrt(1.0 + owner_counts)[:, None]).astype(jnp.bfloat16)
    local_pre = jnp.dot(seed_feats, w_self, preferred_element_type=jnp.float32)
    local_pre = local_pre + jnp.dot(aggregate, w_neigh, preferred_element_type=jnp.float32)
    pre_act = lax.psum(local_pre, "feat")
    hidden = jnp.maximum(pre_act + bias_term, 0.0).astype(jnp.bfloat16)
    grad_rows = jnp.where(hidden > 0, out_grad, jnp.zeros_like(out_grad))
    seed_cols = lax.all_to_all(seed_feats, "node", 1, 0, tiled=True)
    agg_cols = lax.all_to_all(aggregate, "node", 1, 0, tiled=True)
    grad_all = lax.all_gather(grad_rows, "node", axis=0, tiled=True)
    contract_rows = (((0,), (0,)), ((), ()))
    grad_self = lax.dot_general(
        seed_cols, grad_all, contract_rows, preferred_element_type=jnp.float32
    )
    grad_neigh = lax.dot_general(
        agg_cols, grad_all, contract_rows, preferred_element_type=jnp.float32
    )
    hid_chunk = grad_all.shape[1] // n_node
    grad_bias = jnp.sum(
        lax.dynamic_slice_in_dim(grad_all, node_idx * hid_chunk, hid_chunk, axis=1).astype(
            jnp.float32
        ),
        axis=0,
    )
    return (hidden, grad_self, grad_neigh, grad_bias)


def solution(mesh):
    return jax.shard_map(
        body,
        mesh=mesh,
        in_specs=(
            P("node", "feat"),
            P("node", "feat"),
            P("node", None, None, None),
            P("node", None),
            P("node"),
            P("feat", None),
            P("feat", None),
            P(),
            P("node", None),
        ),
        out_specs=(
            P("node", None),
            P(("feat", "node"), None),
            P(("feat", "node"), None),
            P("node"),
        ),
        check_vma=False,
    )
```

```python
import jax
import jax.numpy as jnp
from jax import lax
from jax.sharding import PartitionSpec as P


def unpack(packed):
    shifts = jnp.arange(16, dtype=jnp.int32)
    bit_values = jnp.bitwise_and(jnp.right_shift(packed[..., None], shifts), 1)
    return bit_values.reshape(packed.shape[:-1] + (packed.shape[-1] * 16,)).astype(jnp.bfloat16)


def body(features, seed_feats, patterns, sources, counts, w_self, w_neigh, bias_term, out_grad):
    targets = patterns.shape[0]
    fan_slots = patterns.shape[1]
    block_rows = patterns.shape[2]
    local_blocks = features.shape[0] // block_rows
    n_node = lax.axis_size("node")
    node_idx = lax.axis_index("node")
    live_mask = jnp.arange(fan_slots, dtype=jnp.int32)[None, :] < counts[:, None]
    tile_bits = unpack(patterns) * live_mask[:, :, None, None].astype(jnp.bfloat16)
    source_pick = (
        sources[:, :, None] == jnp.arange(local_blocks, dtype=jnp.int32)[None, None, :]
    ).astype(jnp.bfloat16)
    mixing = jnp.einsum(
        "tkrs,tkb->trbs", tile_bits, source_pick, preferred_element_type=jnp.bfloat16
    )
    mixing = mixing.reshape(targets * block_rows, local_blocks * block_rows)
    feat_cols = features.shape[1]
    with_ones = jnp.concatenate(
        [features, jnp.ones((features.shape[0], 128), features.dtype)], axis=1
    )
    summed_rows = jnp.dot(mixing, with_ones, preferred_element_type=jnp.float32)
    owner_all = lax.psum_scatter(summed_rows, "node", scatter_dimension=0, tiled=True)
    owner_sums = owner_all[:, :feat_cols]
    owner_counts = owner_all[:, feat_cols]
    aggregate = (owner_sums / jnp.sqrt(1.0 + owner_counts)[:, None]).astype(jnp.bfloat16)
    local_pre = jnp.dot(seed_feats, w_self, preferred_element_type=jnp.float32)
    local_pre = local_pre + jnp.dot(aggregate, w_neigh, preferred_element_type=jnp.float32)
    pre_act = lax.psum(local_pre, "feat")
    hidden = jnp.maximum(pre_act + bias_term, 0.0).astype(jnp.bfloat16)
    grad_rows = jnp.where(hidden > 0, out_grad, jnp.zeros_like(out_grad))
    seed_cols = lax.all_to_all(seed_feats, "node", 1, 0, tiled=True)
    agg_cols = lax.all_to_all(aggregate, "node", 1, 0, tiled=True)
    grad_all = lax.all_gather(grad_rows, "node", axis=0, tiled=True)
    contract_rows = (((0,), (0,)), ((), ()))
    grad_self = lax.dot_general(
        seed_cols, grad_all, contract_rows, preferred_element_type=jnp.float32
    )
    grad_neigh = lax.dot_general(
        agg_cols, grad_all, contract_rows, preferred_element_type=jnp.float32
    )
    hid_chunk = grad_all.shape[1] // n_node
    grad_bias = jnp.sum(
        lax.dynamic_slice_in_dim(grad_all, node_idx * hid_chunk, hid_chunk, axis=1).astype(
            jnp.float32
        ),
        axis=0,
    )
    return (hidden, grad_self, grad_neigh, grad_bias)


def solution(mesh):
    return jax.shard_map(
        body,
        mesh=mesh,
        in_specs=(
            P("node", "feat"),
            P("node", "feat"),
            P("node", None, None, None),
            P("node", None),
            P("node"),
            P("feat", None),
            P("feat", None),
            P(),
            P("node", None),
        ),
        out_specs=(
            P("node", None),
            P(("feat", "node"), None),
            P(("feat", "node"), None),
            P("node"),
        ),
        check_vma=False,
    )
```

```python
import jax
import jax.numpy as jnp
from jax import lax
from jax.sharding import PartitionSpec as P


def unpack(packed):
    shifts = jnp.arange(16, dtype=jnp.int32)
    bit_values = jnp.bitwise_and(jnp.right_shift(packed[..., None], shifts), 1)
    return bit_values.reshape(packed.shape[:-1] + (packed.shape[-1] * 16,)).astype(jnp.bfloat16)


def body(features, seed_feats, patterns, sources, counts, w_self, w_neigh, bias_term, out_grad):
    targets = patterns.shape[0]
    fan_slots = patterns.shape[1]
    block_rows = patterns.shape[2]
    local_blocks = features.shape[0] // block_rows
    n_node = lax.axis_size("node")
    node_idx = lax.axis_index("node")
    live_mask = jnp.arange(fan_slots, dtype=jnp.int32)[None, :] < counts[:, None]
    tile_bits = unpack(patterns) * live_mask[:, :, None, None].astype(jnp.bfloat16)
    source_pick = (
        sources[:, :, None] == jnp.arange(local_blocks, dtype=jnp.int32)[None, None, :]
    ).astype(jnp.bfloat16)
    mixing = jnp.einsum(
        "tkrs,tkb->trbs", tile_bits, source_pick, preferred_element_type=jnp.bfloat16
    )
    mixing = mixing.reshape(targets * block_rows, local_blocks * block_rows)
    summed_rows = jnp.dot(mixing, features, preferred_element_type=jnp.float32)
    degree = jnp.sum(mixing, axis=1, dtype=jnp.float32)
    parts = lax.all_to_all(summed_rows, "node", 0, 0, tiled=True)
    owner_rows = parts.shape[0] // n_node
    owner_sums = jnp.sum(parts.reshape(n_node, owner_rows, parts.shape[1]), axis=0)
    owner_counts = lax.psum_scatter(degree, "node", scatter_dimension=0, tiled=True)
    aggregate = (owner_sums / jnp.sqrt(1.0 + owner_counts)[:, None]).astype(jnp.bfloat16)
    local_pre = jnp.dot(seed_feats, w_self, preferred_element_type=jnp.float32)
    local_pre = local_pre + jnp.dot(aggregate, w_neigh, preferred_element_type=jnp.float32)
    pre_act = lax.psum(local_pre, "feat")
    hidden = jnp.maximum(pre_act + bias_term, 0.0).astype(jnp.bfloat16)
    grad_rows = jnp.where(hidden > 0, out_grad, jnp.zeros_like(out_grad))
    seed_cols = lax.all_to_all(seed_feats, "node", 1, 0, tiled=True)
    agg_cols = lax.all_to_all(aggregate, "node", 1, 0, tiled=True)
    grad_all = lax.all_gather(grad_rows, "node", axis=0, tiled=True)
    contract_rows = (((0,), (0,)), ((), ()))
    grad_self = lax.dot_general(
        seed_cols, grad_all, contract_rows, preferred_element_type=jnp.float32
    )
    grad_neigh = lax.dot_general(
        agg_cols, grad_all, contract_rows, preferred_element_type=jnp.float32
    )
    hid_chunk = grad_all.shape[1] // n_node
    grad_bias = jnp.sum(
        lax.dynamic_slice_in_dim(grad_all, node_idx * hid_chunk, hid_chunk, axis=1).astype(
            jnp.float32
        ),
        axis=0,
    )
    return (hidden, grad_self, grad_neigh, grad_bias)


def solution(mesh):
    return jax.shard_map(
        body,
        mesh=mesh,
        in_specs=(
            P("node", "feat"),
            P("node", "feat"),
            P("node", None, None, None),
            P("node", None),
            P("node"),
            P("feat", None),
            P("feat", None),
            P(),
            P("node", None),
        ),
        out_specs=(
            P("node", None),
            P(("feat", "node"), None),
            P(("feat", "node"), None),
            P("node"),
        ),
        check_vma=False,
    )
```
